32 devices in a mesh: mode: 4 (over y, x), space: 8 (over z, core).
Axes of the slice: x: 2, y: 2, z: 4, core: 2. Of those that a mesh axis runs over, the one named last changes fastest.
Arguments:
- resident: bfloat16 [2, 4096, 8, 2048], P(None, 'mode', None, 'space'), may hold values from -0.09375 to 0.09375
- source: bfloat16 [2, 384, 8, 2048], P(None, 'mode', None, 'space'), may hold values from -6 to 6
- insertion: bfloat16 [4, 384, 1024], replicated, may hold values from -0.3125 to 0.3125
- owners: int32 [128, 1], P('mode'), may hold values from 0 to 7; in each aligned block of 32 rows (0 to 31, 32 to 63, ...) at most 4 rows name the same one
- diag_time: int32 [4], replicated, may hold values from 0 to 7
- diag_mom: int32 [4], replicated, may hold values from 1 to 4
Outputs:
- mesons: bfloat16 [32, 2, 512, 1024], P('space', None, 'mode')
The draws below stay inside these ranges and needn't reach their ends.
Inputs may be any that keep to these rules, and one draw needn't show every extreme that they name: `owners`: within the 32 strips of one index of mode, no owner is named more than 4 times.
All inputs are finite; a program needn't handle non-finite values.
Results may differ from the reference program's by a relative error of at most 0.019.
Values may be sent and summed in bfloat16 or wider, within the bound.
A program may use at most 192 MiB of HBM per device.

```python
import math
import jax
import jax.numpy as jnp
import numpy as np
from jax import lax

SRC = 384
RES_DEV = 1024
RES = 4096
STRIP = 128
OUTW = 1024
SLAB = 256
SPACE_SITES = 2048
NT = 8
DIAG = 4
NMOM = 4
LX = 96
CAP = 4
STRIPS_DEV = 32
N_MODE = 4
N_SPACE = 8


def touch_ends(entries, stream_key, low, top_value):
    place = [jax.random.randint(jax.random.fold_in(stream_key, axis), (), 0, length) for axis, length in enumerate(entries.shape)]
    longest = entries.shape.index(max(entries.shape))
    beside = place[:longest] + [(place[longest] + 1) % entries.shape[longest]] + place[longest + 1:]
    return entries.at[tuple(place)].set(low).at[tuple(beside)].set(top_value)


def levels(key, extent, pieces, least, high):
    def one(position, blocks):
        draws = jax.random.uniform(jax.random.fold_in(jax.random.fold_in(key, 6), position), (blocks,), jnp.float32, least / len(pieces), high / len(pieces))
        return jnp.repeat(jnp.exp(draws), extent[position] // blocks).reshape((-1,) + (1,) * (len(extent) - position - 1))

    loudness = one(*pieces[0])
    for cut in pieces[1:]:
        loudness = loudness * one(*cut)
    return loudness


def assign_block(key, own, number, rows, number_of, top, bound, lean):
    order = jax.random.permutation(key, number_of)
    heavy_load, common = portions_of(number_of, rows * top, bound, lean, True), portions_of(number_of, rows * top, bound, lean, False)
    places = jnp.arange(number_of)

    def named(lengths, turn):
        used = int((lengths > 0).sum())
        fixed = max(1, used // 4)
        shifted = fixed + (places - fixed + turn * (used - fixed)) % max(1, number_of - fixed)
        return jnp.zeros((number_of,), jnp.int32).at[order[jnp.where(places < fixed, places, shifted)]].set(jnp.asarray(lengths, jnp.int32))

    lengths = jnp.where(number % 4 == 0, named(heavy_load, number // 4), named(common, number - number // 4 - 1))
    mixed = jax.random.permutation(jax.random.fold_in(own, 3), number_of)
    giver, sink = mixed[0:number_of // 2 * 2:2], mixed[1:number_of // 2 * 2:2]
    room = jnp.minimum(lengths[giver] - 1, bound - lengths[sink]) // 2
    room = jnp.where((giver == order[0]) | (sink == order[0]) | (lengths[sink] == 0), 0, jnp.maximum(room, 0))
    shifted = jax.random.randint(jax.random.fold_in(own, 4), (number_of // 2,), 0, 1 << 20) % (room + 1)
    lengths = lengths.at[giver].add(-shifted).at[sink].add(shifted)
    labels = jnp.searchsorted(jnp.cumsum(lengths), jnp.arange(rows * top), side="right").astype(jnp.int32)
    table = labels.reshape(top, rows).T
    table = table[jax.random.permutation(jax.random.fold_in(own, 1), rows)]
    turn = jax.random.randint(jax.random.fold_in(own, 2), (rows, 1), 0, top)
    return jnp.take_along_axis(table, (jnp.arange(top)[None, :] + turn) % top, axis=1)


def portions_of(number_of, total, reach, slope, full):
    loads = [(1 << 20) // math.isqrt(rank ** slope) + 1 for rank in range(1, number_of + 1)]
    largest = reach if full else min(reach, max(-(-total // number_of), total * loads[0] // sum(loads)))
    least = 1 if total - largest >= number_of - 1 else 0
    given, surplus = [largest] + [least] * (number_of - 1), total - largest - least * (number_of - 1)
    while surplus > 0:
        candidates = [i for i in range(1, number_of) if given[i] < largest] or [i for i in range(1, number_of) if given[i] < reach]
        pool, remaining = sum([loads[i] for i in candidates]), surplus
        for i in candidates:
            extra = min(reach - given[i], max(1, remaining * loads[i] // pool), surplus)
            given[i] = given[i] + extra
            surplus = surplus - extra
    return np.array(given)


def noise(own_key, dims, width, most, pieces=(), held_as=jnp.bfloat16):
    entries = jax.random.normal(own_key, dims, jnp.float32) * width
    if len(pieces) > 0:
        entries = levels(own_key, dims, pieces, -0.22, 0.18) * entries
    return jnp.clip(entries, min=-most, max=most).astype(held_as)


def setup_inputs(seed: int = 0) -> dict:
    seeds = jax.random.split(jax.random.key(seed), 7)
    resident = noise(seeds[0], (2, RES, NT, SPACE_SITES), (2 * SLAB * N_SPACE) ** -0.5, 0.09375, ((1, 4), (3, 8)))
    source = noise(seeds[1], (2, SRC, NT, SPACE_SITES), 1.0, 6.0, ((1, 4), (3, 8)))
    insertion = noise(seeds[2], (DIAG, SRC, OUTW), SRC ** -0.5, 0.3125)
    owners_keys = jax.random.split(jax.random.fold_in(seeds[3], 1), (N_MODE * STRIPS_DEV) // STRIPS_DEV)
    owners_turns = jax.random.permutation(jax.random.fold_in(seeds[3], 3), (N_MODE * STRIPS_DEV) // STRIPS_DEV)
    owners = jax.vmap(lambda own, number: assign_block(jax.random.fold_in(seeds[3], 2), own, number, STRIPS_DEV, N_SPACE, 1, CAP, 2))(owners_keys, owners_turns).reshape((N_MODE * STRIPS_DEV, 1))
    diag_time = touch_ends(jax.random.randint(seeds[4], (DIAG,), 0, NT), jax.random.fold_in(seeds[4], 1), 0, NT - 1).astype(jnp.int32)
    diag_mom = touch_ends(jax.random.randint(seeds[5], (DIAG,), 1, NMOM + 1), jax.random.fold_in(seeds[5], 1), 1, NMOM).astype(jnp.int32)
    return {"resident": resident, "source": source, "insertion": insertion, "owners": owners, "diag_time": diag_time, "diag_mom": diag_mom}


def phase_pair(momentum, start, count):
    lattice_positions = (start + jnp.arange(count, dtype=jnp.int32)) % LX
    turns = (momentum * lattice_positions) % LX
    angle = (2.0 * math.pi / LX) * turns.astype(jnp.float32)
    return jnp.cos(angle), jnp.sin(angle)


def one_field(res_slice, src_slice, momentum):
    def accumulate_portion(total, shard):
        start = (shard * SLAB).astype(jnp.int32)
        res_part = lax.dynamic_slice_in_dim(res_slice, start, SLAB, 2).astype(jnp.float32)
        src_part = lax.dynamic_slice_in_dim(src_slice, start, SLAB, 2)
        cosine, sine = phase_pair(momentum, start, SLAB)
        real_in = res_part[0] * cosine[None, :] - res_part[1] * sine[None, :]
        imag_in = -(res_part[0] * sine[None, :] + res_part[1] * cosine[None, :])
        phased = jnp.stack([real_in, imag_in]).astype(jnp.bfloat16)
        combos = jnp.einsum("prx,qsx->pqrs", phased.astype(jnp.float32), src_part.astype(jnp.float32))
        real_out = combos[0, 0] - combos[1, 1]
        imag_out = combos[0, 1] + combos[1, 0]
        term = jnp.stack([real_out, imag_out]).astype(jnp.bfloat16)
        term = lax.optimization_barrier(term)
        return total + term.astype(jnp.float32), None

    total, unused = lax.scan(accumulate_portion, jnp.zeros((2, RES, SRC), jnp.float32), jnp.arange(N_SPACE, dtype=jnp.int32))
    return total.astype(jnp.bfloat16)


def reference(resident, source, insertion, owners, diag_time, diag_mom):
    fields = []
    for diagram in range(DIAG):
        res_slice = jnp.take(resident, diag_time[diagram], axis=2)
        src_slice = jnp.take(source, diag_time[diagram], axis=2)
        fields.append(one_field(res_slice, src_slice, diag_mom[diagram]))
    field = jnp.stack(fields)
    blocks = RES_DEV // STRIP
    band_list = field.reshape(DIAG, 2, N_MODE, blocks, STRIP, SRC).transpose(2, 0, 3, 1, 4, 5)
    band_list = band_list.reshape(N_MODE, STRIPS_DEV, 2, STRIP, SRC)
    strip_diag = jnp.arange(STRIPS_DEV, dtype=jnp.int32) // blocks
    selected_targets = jnp.take(insertion, strip_diag, axis=0)
    product = jnp.einsum("mkpas,kso->mkpao", band_list.astype(jnp.float32), selected_targets.astype(jnp.float32)).astype(jnp.bfloat16)
    owner_list = owners[:, 0].reshape(N_MODE, STRIPS_DEV)
    same = owner_list[:, :, None] == owner_list[:, None, :]
    order = jnp.arange(STRIPS_DEV, dtype=jnp.int32)
    earlier = order[None, :] < order[:, None]
    rank = jnp.sum((same & earlier[None, :, :]).astype(jnp.int32), axis=2)
    slot = owner_list * CAP + rank
    mode_grid = jnp.broadcast_to(jnp.arange(N_MODE, dtype=jnp.int32)[:, None], (N_MODE, STRIPS_DEV))
    mesons = jnp.zeros((N_SPACE * CAP, N_MODE, 2, STRIP, OUTW), jnp.bfloat16)
    mesons = mesons.at[slot, mode_grid].set(product)
    return mesons.transpose(0, 2, 1, 3, 4).reshape(N_SPACE * CAP, 2, N_MODE * STRIP, OUTW)
```

```python
import functools
import math

import jax
import jax.numpy as jnp
from jax import lax
from jax.experimental import pallas as pl
from jax.experimental.pallas import tpu as pltpu
from jax.sharding import PartitionSpec as P

STRIP = 128
LX = 96
CAP = 4
AHEAD = 3
PICK = 32
VMEM = 67043328
SPARE = 1 << 20
MESH = pl.DeviceIdType.MESH


def wrapped(count):
    return count - LX * jnp.floor((count + 0.5) * (1.0 / LX))


def phase_pair(mom_ref, start, diagrams, count):
    row = lax.broadcasted_iota(jnp.int32, (diagrams, count), 0)
    site = lax.broadcasted_iota(jnp.int32, (diagrams, count), 1) + start % LX
    momentum = jnp.zeros((diagrams, count), jnp.int32)
    for d in range(diagrams):
        momentum = jnp.where(row == d, mom_ref[d], momentum)
    turns = wrapped(momentum.astype(jnp.float32) * wrapped(site.astype(jnp.float32)))
    angle = 2.0 * math.pi / LX * turns
    return (jnp.cos(angle), jnp.sin(angle))


def fill_slots(owner_ref, strip_ref, n_space):
    count = owner_ref.shape[0]
    bits = (count - 1).bit_length()

    def of_owner(o, carry):
        packed, unit = jnp.int32(0), jnp.int32(1)
        for k in range(count):
            named = owner_ref[k] == o
            packed = jnp.where(named, packed + k * unit, packed)
            unit = jnp.where(named, unit * (1 << bits), unit)
        for c in range(CAP):
            strip_ref[o * CAP + c] = packed // (1 << bits * c) % (1 << bits)
        return carry

    lax.fori_loop(0, n_space, of_owner, 0)


def pick_rows(rows, times, time):
    row = lax.broadcasted_iota(jnp.int32, (rows, rows * times), 0)
    col = lax.broadcasted_iota(jnp.int32, (rows, rows * times), 1)
    return jnp.where(col == row * times + time, 1.0, 0.0).astype(jnp.bfloat16)


def field_kernel(
    n_mode, n_space, blocks, times, depth, time_hbm, mom_hbm, owner_hbm, res_hbm, src_hbm, ins_hbm, out_ref, *scratch
):
    others = scratch[:n_mode - 1]
    (a_ref, s_ref, pick, res_buf, src_buf, ins, mine, theirs, came, acc, field, cos_ref, sin_ref,
     time_ref, mom_ref, owner_ref, strip_ref,
     small_sem, src_sem, res_sem, ins_sem, gs_sem, gr_sem, ps_sem, pr_sem, zs_sem, zr_sem) = scratch[n_mode - 1:]
    diagrams = s_ref.shape[0]
    chunk = STRIP * times
    sources = (s_ref,) + others
    src_dev = s_ref.shape[1] // 2
    n_line = n_space // 2
    steps = n_line * CAP
    me = lax.axis_index("space")
    mode = lax.axis_index("mode")
    z, core = me // 2, me % 2
    partner = z * 2 + 1 - core

    barrier = pltpu.get_barrier_semaphore()

    def greet(space, other_mode):
        pl.semaphore_signal(barrier, inc=1, device_id=(other_mode, space), device_id_type=MESH)

    def other_mode(q, sign):
        if n_mode & (n_mode - 1):
            return (mode + n_mode + sign * q) % n_mode
        there, bit = 0, 1
        while bit < n_mode:
            ours = mode // bit % 2
            there += bit * (1 - ours if q & bit else ours)
            bit *= 2
        return there

    def fetch(b):
        rows = pl.ds(pl.multiple_of(b * chunk, chunk), chunk)
        return pltpu.make_async_copy(res_hbm.at[:, rows, :], res_buf.at[b % depth], res_sem.at[b % depth])

    src_copy = pltpu.make_async_copy(src_hbm, src_buf, src_sem)
    ins_copy = pltpu.make_async_copy(ins_hbm, ins, ins_sem)
    small = [
        pltpu.make_async_copy(there, here, small_sem.at[i])
        for i, (there, here) in enumerate(((time_hbm, time_ref), (mom_hbm, mom_ref), (owner_hbm, owner_ref)))
    ]
    for copy in small:
        copy.start()
    src_copy.start()
    for b in range(depth):
        fetch(b).start()
    greet(partner, mode)

    @pl.when(z > 0)
    def _():
        greet(me - 2, mode)

    @pl.when(z < n_line - 1)
    def _():
        greet(me + 2, mode)

    for q in range(1, n_mode):
        greet(me, other_mode(q, 1))

    taken = PICK * times
    for copy in small:
        copy.wait()
    for d in range(diagrams):
        pick[d * PICK:(d + 1) * PICK, :] = pick_rows(PICK, times, time_ref[d])
    fill_slots(owner_ref, strip_ref, n_space)
    cos_ref[...], sin_ref[...] = phase_pair(mom_ref, me * cos_ref.shape[1], diagrams, cos_ref.shape[1])
    src_copy.wait()
    for part in range(src_dev // PICK):
        for p in range(2):
            chosen = jnp.dot(
                pick[...], src_buf[p, part * taken:(part + 1) * taken, :],
                preferred_element_type=jnp.float32,
            ).astype(jnp.bfloat16)
            first = p * src_dev + part * PICK
            for d in range(diagrams):
                s_ref[d, first:first + PICK, :] = chosen[d * PICK:(d + 1) * PICK]
    pl.semaphore_wait(barrier, n_mode + jnp.minimum(z, 1) + jnp.minimum(n_line - 1 - z, 1))

    def gather(q):
        return pltpu.make_async_remote_copy(
            src_ref=s_ref, dst_ref=others[q - 1], send_sem=gs_sem.at[q - 1], recv_sem=gr_sem.at[q - 1],
            device_id=(other_mode(q, -1), me), device_id_type=MESH,
        )

    for q in range(1, n_mode):
        gather(q).start()

    def phase(b, carry):
        fetch(b).wait()
        for part in range(STRIP // PICK):
            span = slice(part * taken, (part + 1) * taken)
            real = jnp.dot(pick[...], res_buf[b % depth, 0, span, :], preferred_element_type=jnp.float32)
            imag = jnp.dot(pick[...], res_buf[b % depth, 1, span, :], preferred_element_type=jnp.float32)
            for d in range(diagrams):
                own = slice(d * PICK, (d + 1) * PICK)
                cosine, sine = cos_ref[d:d + 1, :], sin_ref[d:d + 1, :]
                first = part * PICK
                a_ref[d * blocks + b, first:first + PICK, :] = (
                    real[own] * cosine - imag[own] * sine
                ).astype(jnp.bfloat16)
                a_ref[d * blocks + b, STRIP + first:STRIP + first + PICK, :] = (
                    -(real[own] * sine + imag[own] * cosine)
                ).astype(jnp.bfloat16)

        @pl.when(b + depth < blocks)
        def _():
            fetch(b + depth).start()

        return carry

    lax.fori_loop(0, blocks, phase, 0)
    ins_copy.start()

    def place(k):
        s, j = k // CAP, k % CAP
        low = z < n_line // 2
        near = jnp.where(low, z, n_line - 1 - z)
        turn = s // 2
        t = jnp.where(s < 2 * near, turn + (1 - s % 2) * (n_line - 1 - 2 * turn), n_line - 1 - (s - near))
        return jnp.where(low, t, n_line - 1 - t) * CAP + j

    def term(slot, source):
        strip = strip_ref[slot]
        both = lax.dot_general(
            source[strip // blocks], a_ref[strip], (((1,), (1,)), ((), ())),
            preferred_element_type=jnp.float32,
        )
        real = both[:src_dev, :STRIP] - both[src_dev:, STRIP:]
        imag = both[src_dev:, :STRIP] + both[:src_dev, STRIP:]
        return real, imag

    def across(line_slot, q):
        return pltpu.make_async_remote_copy(
            src_ref=theirs.at[line_slot, q], dst_ref=mine.at[line_slot, q],
            send_sem=ps_sem.at[line_slot, q], recv_sem=pr_sem.at[line_slot, q],
            device_id=(mode, partner), device_id_type=MESH,
        )

    def along(line_slot, landing, q, step):
        return pltpu.make_async_remote_copy(
            src_ref=mine.at[line_slot, q], dst_ref=came.at[landing, q],
            send_sem=zs_sem.at[line_slot, q], recv_sem=zr_sem.at[landing, q],
            device_id=(mode, me + step), device_id_type=MESH,
        )

    def slot_of(line_slot, its_core):
        return (line_slot // CAP * 2 + its_core) * CAP + line_slot % CAP

    def give(line_slot, q):
        real, imag = term(slot_of(line_slot, 1 - core), sources[q])
        theirs[line_slot, q, :src_dev, :] = real.astype(jnp.bfloat16)
        theirs[line_slot, q, src_dev:, :] = imag.astype(jnp.bfloat16)
        across(line_slot, q).start()

    def sum_of_chip(line_slot, q):
        real, imag = term(slot_of(line_slot, core), sources[q])
        across(line_slot, q).wait_recv()
        acc[:src_dev, :] = real + mine[line_slot, q, :src_dev, :].astype(jnp.float32)
        acc[src_dev:, :] = imag + mine[line_slot, q, src_dev:, :].astype(jnp.float32)

    def add_arrival(landing, q):
        along(0, landing, q, 0).wait_recv()
        acc[...] += came[landing, q].astype(jnp.float32)

    def run(count, order, body, q):
        def first(k, carry):
            give(order(k), q)
            return carry

        def step(k, carry):
            @pl.when(k + AHEAD < count)
            def _():
                give(order(k + AHEAD), q)

            body(order(k), q)
            return carry

        lax.fori_loop(0, min(AHEAD, count), first, 0)
        lax.fori_loop(0, count, step, 0)

    def transit(line_slot, q):
        t = line_slot // CAP
        sum_of_chip(line_slot, q)

        @pl.when((t > z) & (z > 0))
        def _():
            add_arrival(line_slot + CAP, q)

        @pl.when((t < z) & (z < n_line - 1))
        def _():
            add_arrival(line_slot, q)

        mine[line_slot, q] = acc[...].astype(jnp.bfloat16)

        @pl.when(t > z)
        def _():
            along(line_slot, line_slot + CAP, q, 2).start()

        @pl.when(t < z)
        def _():
            along(line_slot, line_slot, q, -2).start()

    def arrive(line_slot, q):
        j = line_slot % CAP
        sum_of_chip(line_slot, q)

        @pl.when(z > 0)
        def _():
            add_arrival(line_slot + CAP, q)

        @pl.when(z < n_line - 1)
        def _():
            add_arrival(line_slot, q)

        rows = pl.ds(pl.multiple_of(other_mode(q, 1) * src_dev, 16), src_dev)
        field[j, rows, :STRIP] = acc[:src_dev, :].astype(jnp.bfloat16)
        field[j, rows, STRIP:] = acc[src_dev:, :].astype(jnp.bfloat16)
        if q == n_mode - 1:
            product = lax.dot_general(
                field[j], ins[strip_ref[slot_of(line_slot, core)] // blocks], (((0,), (0,)), ((), ())),
                preferred_element_type=jnp.float32,
            )
            out_ref[j] = product.astype(jnp.bfloat16)

    for q in range(n_mode + 1):
        if 0 < q < n_mode:
            gather(q).wait_recv()
        if q < n_mode:
            run(steps - CAP, place, transit, q)
        if q == n_mode:
            ins_copy.wait()
        if q > 0:
            run(CAP, lambda k: z * CAP + k, arrive, q - 1)

    for q in range(1, n_mode):
        gather(q).wait_send()

    def drain(line_slot, carry):
        for q in range(n_mode):
            across(line_slot, q).wait_send()

            @pl.when(line_slot // CAP != z)
            def _(q=q):
                along(line_slot, line_slot, q, 0).wait_send()
        return carry

    lax.fori_loop(0, steps, drain, 0)


def on_device(resident, source, insertion, owners, diag_time, diag_mom):
    _, res_dev, times, slab = resident.shape
    src_dev = source.shape[1]
    n_mode = lax.axis_size("mode")
    n_space = lax.axis_size("space")
    diagrams, src, width = insertion.shape
    blocks = res_dev // STRIP
    strip_count = diagrams * blocks
    slots = n_space * CAP
    me_space = lax.axis_index("space")
    owner_list = owners[:, 0]

    bf16 = jnp.bfloat16
    steps = n_space // 2 * CAP
    piece = (n_mode, 2 * src_dev, STRIP)
    dma = pltpu.SemaphoreType.DMA
    vmem = pl.BlockSpec(memory_space=pltpu.VMEM)
    hbm = pl.BlockSpec(memory_space=pltpu.HBM)
    buffers = [pltpu.VMEM((diagrams, 2 * src_dev, slab), bf16)] * (n_mode - 1) + [
        pltpu.VMEM((strip_count, 2 * STRIP, slab), bf16),
        pltpu.VMEM((diagrams, 2 * src_dev, slab), bf16),
        pltpu.VMEM((diagrams * PICK, PICK * times), bf16),
        None,
        pltpu.VMEM((2, src_dev * times, slab), bf16),
        pltpu.VMEM((diagrams, src, width), bf16),
        pltpu.VMEM((steps,) + piece, bf16),
        pltpu.VMEM((steps,) + piece, bf16),
        pltpu.VMEM((steps + CAP,) + piece, bf16),
        pltpu.VMEM((2 * src_dev, STRIP), jnp.float32),
        pltpu.VMEM((CAP, src, 2 * STRIP), bf16),
        pltpu.VMEM((diagrams, slab), jnp.float32),
        pltpu.VMEM((diagrams, slab), jnp.float32),
        pltpu.SMEM((diagrams,), jnp.int32),
        pltpu.SMEM((diagrams,), jnp.int32),
        pltpu.SMEM((strip_count,), jnp.int32),
        pltpu.SMEM((slots,), jnp.int32),
    ]
    block = pltpu.VMEM((1, 2, STRIP * times, slab), bf16)
    held = [math.prod(b.shape) * b.dtype.itemsize for b in buffers + [block] if b is not None]
    limit = VMEM - CAP * 2 * STRIP * width * 2 - SPARE // 4
    depth = max(2, min(blocks, (limit - SPARE - sum(held[:-1])) // held[-1]))
    buffers[n_mode + 2] = pltpu.VMEM((depth, 2, STRIP * times, slab), bf16)
    semaphores = [
        dma((3,)),
        dma(()),
        dma((depth,)),
        dma(()),
        dma((n_mode - 1,)),
        dma((n_mode - 1,)),
        dma((steps, n_mode)),
        dma((steps, n_mode)),
        dma((steps, n_mode)),
        dma((steps + CAP, n_mode)),
    ]
    mesons = pl.pallas_call(
        functools.partial(field_kernel, n_mode, n_space, blocks, times, depth),
        in_specs=[hbm] * 6,
        out_specs=vmem,
        out_shape=pltpu.VMEM((CAP, 2 * STRIP, width), bf16),
        scratch_shapes=buffers + semaphores,
        compiler_params=pltpu.CompilerParams(
            collective_id=0, has_side_effects=True, vmem_limit_bytes=limit
        ),
        name="field",
    )(
        diag_time, diag_mom, owner_list, resident.reshape(2, res_dev * times, slab),
        source.reshape(2, src_dev * times, slab), insertion,
    )
    mesons = mesons.reshape(CAP, 2, STRIP, width)
    if strip_count < slots:
        taken = jnp.sum((owner_list == me_space).astype(jnp.int32))
        filled = jnp.arange(CAP, dtype=jnp.int32) < taken
        mesons = jnp.where(filled[:, None, None, None], mesons, jnp.zeros_like(mesons))
    return mesons


def solution(mesh):
    in_specs = (
        P(None, "mode", None, "space"),
        P(None, "mode", None, "space"),
        P(),
        P("mode", None),
        P(),
        P(),
    )
    out_specs = P("space", None, "mode", None)
    return jax.shard_map(
        on_device, mesh=mesh, in_specs=in_specs, out_specs=out_specs, check_vma=False
    )
```

```python
import functools
import math

import jax
import jax.numpy as jnp
from jax import lax
from jax.experimental import pallas as pl
from jax.experimental.pallas import tpu as pltpu
from jax.sharding import PartitionSpec as P

STRIP = 128
LX = 96
CAP = 4
AHEAD = 4
RING = 2 * AHEAD + 2
WAVES = (2, 2, 1, 1)
PICK = 32
VMEM = 67043328
SPARE = 1 << 20
MESH = pl.DeviceIdType.MESH


def wrapped(count):
    return count - LX * jnp.floor((count + 0.5) * (1.0 / LX))


def phase_pair(mom_ref, start, diagrams, count):
    row = lax.broadcasted_iota(jnp.int32, (diagrams, count), 0)
    site = lax.broadcasted_iota(jnp.int32, (diagrams, count), 1) + start % LX
    momentum = jnp.zeros((diagrams, count), jnp.int32)
    for d in range(diagrams):
        momentum = jnp.where(row == d, mom_ref[d], momentum)
    turns = wrapped(momentum.astype(jnp.float32) * wrapped(site.astype(jnp.float32)))
    angle = 2.0 * math.pi / LX * turns
    return (jnp.cos(angle), jnp.sin(angle))


def fill_slots(owner_ref, strip_ref, n_space):
    count = owner_ref.shape[0]
    bits = (count - 1).bit_length()

    def of_owner(o, carry):
        packed, unit = jnp.int32(0), jnp.int32(1)
        for k in range(count):
            named = owner_ref[k] == o
            packed = jnp.where(named, packed + k * unit, packed)
            unit = jnp.where(named, unit * (1 << bits), unit)
        for c in range(CAP):
            strip_ref[o * CAP + c] = packed // (1 << bits * c) % (1 << bits)
        return carry

    lax.fori_loop(0, n_space, of_owner, 0)


def pick_rows(rows, times, time):
    row = lax.broadcasted_iota(jnp.int32, (rows, rows * times), 0)
    col = lax.broadcasted_iota(jnp.int32, (rows, rows * times), 1)
    return jnp.where(col == row * times + time, 1.0, 0.0).astype(jnp.bfloat16)


def field_kernel(
    n_mode, n_space, blocks, times, depth, time_hbm, mom_hbm, owner_hbm, res_hbm, src_hbm, ins_hbm, out_ref, *scratch
):
    others = scratch[:n_mode - 1]
    (a_ref, s_ref, pick, res_buf, src_buf, ins, mine, theirs, came, acc, field, cos_ref, sin_ref,
     time_ref, mom_ref, owner_ref, strip_ref,
     small_sem, src_sem, res_sem, ins_sem, gs_sem, gr_sem, ps_sem, pr_sem, zs_sem, zr_sem) = scratch[n_mode - 1:]
    diagrams = s_ref.shape[0]
    chunk = STRIP * times
    sources = (s_ref,) + others
    src_dev = s_ref.shape[1] // 2
    n_line = n_space // 2
    steps = n_line * CAP
    me = lax.axis_index("space")
    mode = lax.axis_index("mode")
    z, core = me // 2, me % 2
    partner = z * 2 + 1 - core

    barrier = pltpu.get_barrier_semaphore()

    def greet(space, other_mode):
        pl.semaphore_signal(barrier, inc=1, device_id=(other_mode, space), device_id_type=MESH)

    def other_mode(q, sign):
        if n_mode & (n_mode - 1):
            return (mode + n_mode + sign * q) % n_mode
        there, bit = 0, 1
        while bit < n_mode:
            ours = mode // bit % 2
            there += bit * (1 - ours if q & bit else ours)
            bit *= 2
        return there

    def fetch(b):
        rows = pl.ds(pl.multiple_of(b * chunk, chunk), chunk)
        return pltpu.make_async_copy(res_hbm.at[:, rows, :], res_buf.at[b % depth], res_sem.at[b % depth])

    src_copy = pltpu.make_async_copy(src_hbm, src_buf, src_sem)
    ins_copy = pltpu.make_async_copy(ins_hbm, ins, ins_sem)
    small = [
        pltpu.make_async_copy(there, here, small_sem.at[i])
        for i, (there, here) in enumerate(((time_hbm, time_ref), (mom_hbm, mom_ref), (owner_hbm, owner_ref)))
    ]
    for copy in small:
        copy.start()
    src_copy.start()
    flight = min(sum(WAVES), depth)

    def wave(n):
        for b in range(sum(WAVES[:n]), min(sum(WAVES[:n + 1]), flight)):
            fetch(b).start()

    wave(0)
    greet(partner, mode)

    @pl.when(z > 0)
    def _():
        greet(me - 2, mode)

    @pl.when(z < n_line - 1)
    def _():
        greet(me + 2, mode)

    for q in range(1, n_mode):
        greet(me, other_mode(q, 1))

    taken = PICK * times
    for copy in small:
        copy.wait()
    wave(1)
    for d in range(diagrams):
        pick[d * PICK:(d + 1) * PICK, :] = pick_rows(PICK, times, time_ref[d])
    fill_slots(owner_ref, strip_ref, n_space)
    cos_ref[...], sin_ref[...] = phase_pair(mom_ref, me * cos_ref.shape[1], diagrams, cos_ref.shape[1])
    src_copy.wait()
    wave(2)
    for part in range(src_dev // PICK):
        for p in range(2):
            chosen = jnp.dot(
                pick[...], src_buf[p, part * taken:(part + 1) * taken, :],
                preferred_element_type=jnp.float32,
            ).astype(jnp.bfloat16)
            first = p * src_dev + part * PICK
            for d in range(diagrams):
                s_ref[d, first:first + PICK, :] = chosen[d * PICK:(d + 1) * PICK]
    wave(3)

    def phase(b, carry):
        fetch(b).wait()
        for part in range(STRIP // PICK):
            span = slice(part * taken, (part + 1) * taken)
            real = jnp.dot(pick[...], res_buf[b % depth, 0, span, :], preferred_element_type=jnp.float32)
            imag = jnp.dot(pick[...], res_buf[b % depth, 1, span, :], preferred_element_type=jnp.float32)
            for d in range(diagrams):
                own = slice(d * PICK, (d + 1) * PICK)
                cosine, sine = cos_ref[d:d + 1, :], sin_ref[d:d + 1, :]
                first = part * PICK
                a_ref[d * blocks + b, first:first + PICK, :] = (
                    real[own] * cosine - imag[own] * sine
                ).astype(jnp.bfloat16)
                a_ref[d * blocks + b, STRIP + first:STRIP + first + PICK, :] = (
                    -(real[own] * sine + imag[own] * cosine)
                ).astype(jnp.bfloat16)

        @pl.when(b + flight < blocks)
        def _():
            fetch(b + flight).start()

        return carry

    lax.fori_loop(0, blocks, phase, 0)
    pl.semaphore_wait(barrier, n_mode + jnp.minimum(z, 1) + jnp.minimum(n_line - 1 - z, 1))

    def gather(q):
        return pltpu.make_async_remote_copy(
            src_ref=s_ref, dst_ref=others[q - 1], send_sem=gs_sem.at[q - 1], recv_sem=gr_sem.at[q - 1],
            device_id=(other_mode(q, -1), me), device_id_type=MESH,
        )

    for q in range(1, n_mode):
        gather(q).start()

    ins_copy.start()

    def place(k):
        s, j = k // CAP, k % CAP
        low = z < n_line // 2
        near = jnp.where(low, z, n_line - 1 - z)
        turn = s // 2
        t = jnp.where(s < 2 * near, turn + (1 - s % 2) * (n_line - 1 - 2 * turn), n_line - 1 - (s - near))
        return jnp.where(low, t, n_line - 1 - t) * CAP + j

    def term(slot, source):
        strip = strip_ref[slot]
        both = lax.dot_general(
            source[strip // blocks], a_ref[strip], (((1,), (1,)), ((), ())),
            preferred_element_type=jnp.float32,
        )
        real = both[:src_dev, :STRIP] - both[src_dev:, STRIP:]
        imag = both[src_dev:, :STRIP] + both[:src_dev, STRIP:]
        return real, imag

    def across(line_slot, q, turn):
        return pltpu.make_async_remote_copy(
            src_ref=theirs.at[line_slot, q], dst_ref=mine.at[line_slot, q],
            send_sem=ps_sem, recv_sem=pr_sem.at[turn % RING],
            device_id=(mode, partner), device_id_type=MESH,
        )

    def arrival(landing, q):
        if q < n_mode - 1:
            return q * (n_line + 1) + landing // CAP
        return q * (n_line + 1) + landing

    def group(landing):
        near = pl.ds(0, CAP)
        return pltpu.make_async_remote_copy(
            src_ref=came.at[0, near], dst_ref=came.at[0, near], send_sem=zs_sem, recv_sem=zr_sem.at[landing],
            device_id=(mode, partner), device_id_type=MESH,
        )

    def along(line_slot, landing, q, step):
        return pltpu.make_async_remote_copy(
            src_ref=mine.at[line_slot, q], dst_ref=came.at[q, landing],
            send_sem=zs_sem, recv_sem=zr_sem.at[arrival(landing, q)],
            device_id=(mode, me + step), device_id_type=MESH,
        )

    def slot_of(line_slot, its_core):
        return (line_slot // CAP * 2 + its_core) * CAP + line_slot % CAP

    def give(line_slot, q, turn):
        real, imag = term(slot_of(line_slot, 1 - core), sources[q])
        theirs[line_slot, q, :src_dev, :] = real.astype(jnp.bfloat16)
        theirs[line_slot, q, src_dev:, :] = imag.astype(jnp.bfloat16)
        across(line_slot, q, turn).start()

    def sum_of_chip(line_slot, q, turn):
        real, imag = term(slot_of(line_slot, core), sources[q])
        across(line_slot, q, turn).wait_recv()
        acc[:src_dev, :] = real + mine[line_slot, q, :src_dev, :].astype(jnp.float32)
        acc[src_dev:, :] = imag + mine[line_slot, q, src_dev:, :].astype(jnp.float32)

    def add_arrival(landing, q):
        if q < n_mode - 1:
            @pl.when(landing % CAP == 0)
            def _():
                group(arrival(landing, q)).wait_recv()
        else:
            along(0, landing, q, 0).wait_recv()
        acc[...] += came[q, landing].astype(jnp.float32)

    def run(count, order, body, q, turn):
        def first(k, carry):
            give(order(k), q, turn + k)
            return carry

        def step(k, carry):
            @pl.when(k + AHEAD < count)
            def _():
                give(order(k + AHEAD), q, turn + k + AHEAD)

            body(order(k), q, turn + k)
            return carry

        lax.fori_loop(0, min(AHEAD, count), first, 0)
        lax.fori_loop(0, count, step, 0)

    def transit(line_slot, q, turn):
        t = line_slot // CAP
        sum_of_chip(line_slot, q, turn)

        @pl.when((t > z) & (z > 0))
        def _():
            add_arrival(line_slot + CAP, q)

        @pl.when((t < z) & (z < n_line - 1))
        def _():
            add_arrival(line_slot, q)

        mine[line_slot, q] = acc[...].astype(jnp.bfloat16)

        @pl.when(t > z)
        def _():
            along(line_slot, line_slot + CAP, q, 2).start()

        @pl.when(t < z)
        def _():
            along(line_slot, line_slot, q, -2).start()

    def arrive(line_slot, q, turn):
        j = line_slot % CAP
        sum_of_chip(line_slot, q, turn)

        @pl.when(z > 0)
        def _():
            add_arrival(line_slot + CAP, q)

        @pl.when(z < n_line - 1)
        def _():
            add_arrival(line_slot, q)

        rows = pl.ds(pl.multiple_of(other_mode(q, 1) * src_dev, 16), src_dev)
        field[j, rows, :STRIP] = acc[:src_dev, :].astype(jnp.bfloat16)
        field[j, rows, STRIP:] = acc[src_dev:, :].astype(jnp.bfloat16)
        if q == n_mode - 1:
            product = lax.dot_general(
                field[j], ins[strip_ref[slot_of(line_slot, core)] // blocks], (((0,), (0,)), ((), ())),
                preferred_element_type=jnp.float32,
            )
            out_ref[j] = product.astype(jnp.bfloat16)

    turn = 0
    for q in range(n_mode + 1):
        if 0 < q < n_mode:
            gather(q).wait_recv()
        if q < n_mode:
            run(steps - CAP, place, transit, q, turn)
            turn += steps - CAP
        if q == n_mode:
            ins_copy.wait()
        if q > 0:
            run(CAP, lambda k: z * CAP + k, arrive, q - 1, turn)
            turn += CAP

    for q in range(1, n_mode):
        gather(q).wait_send()
    everything = pltpu.make_async_remote_copy(
        src_ref=theirs, dst_ref=mine, send_sem=ps_sem, recv_sem=pr_sem.at[0],
        device_id=(mode, partner), device_id_type=MESH,
    )
    everything.wait_send()
    sent = pl.ds(0, steps - CAP)
    passed_on = pltpu.make_async_remote_copy(
        src_ref=theirs.at[sent], dst_ref=mine.at[sent], send_sem=zs_sem, recv_sem=pr_sem.at[0],
        device_id=(mode, partner), device_id_type=MESH,
    )
    passed_on.wait_send()


def on_device(resident, source, insertion, owners, diag_time, diag_mom):
    _, res_dev, times, slab = resident.shape
    src_dev = source.shape[1]
    n_mode = lax.axis_size("mode")
    n_space = lax.axis_size("space")
    diagrams, src, width = insertion.shape
    blocks = res_dev // STRIP
    strip_count = diagrams * blocks
    slots = n_space * CAP
    me_space = lax.axis_index("space")
    owner_list = owners[:, 0]

    bf16 = jnp.bfloat16
    steps = n_space // 2 * CAP
    piece = (n_mode, 2 * src_dev, STRIP)
    dma = pltpu.SemaphoreType.DMA
    vmem = pl.BlockSpec(memory_space=pltpu.VMEM)
    hbm = pl.BlockSpec(memory_space=pltpu.HBM)
    buffers = [pltpu.VMEM((diagrams, 2 * src_dev, slab), bf16)] * (n_mode - 1) + [
        pltpu.VMEM((strip_count, 2 * STRIP, slab), bf16),
        pltpu.VMEM((diagrams, 2 * src_dev, slab), bf16),
        pltpu.VMEM((diagrams * PICK, PICK * times), bf16),
        None,
        pltpu.VMEM((2, src_dev * times, slab), bf16),
        pltpu.VMEM((diagrams, src, width), bf16),
        pltpu.VMEM((steps,) + piece, bf16),
        pltpu.VMEM((steps,) + piece, bf16),
        pltpu.VMEM((n_mode, steps + CAP) + piece[1:], bf16),
        pltpu.VMEM((2 * src_dev, STRIP), jnp.float32),
        pltpu.VMEM((CAP, src, 2 * STRIP), bf16),
        pltpu.VMEM((diagrams, slab), jnp.float32),
        pltpu.VMEM((diagrams, slab), jnp.float32),
        pltpu.SMEM((diagrams,), jnp.int32),
        pltpu.SMEM((diagrams,), jnp.int32),
        pltpu.SMEM((strip_count,), jnp.int32),
        pltpu.SMEM((slots,), jnp.int32),
    ]
    block = pltpu.VMEM((1, 2, STRIP * times, slab), bf16)
    held = [math.prod(b.shape) * b.dtype.itemsize for b in buffers + [block] if b is not None]
    limit = VMEM - CAP * 2 * STRIP * width * 2 - SPARE // 4
    depth = max(2, min(blocks, (limit - SPARE - sum(held[:-1])) // held[-1]))
    buffers[n_mode + 2] = pltpu.VMEM((depth, 2, STRIP * times, slab), bf16)
    semaphores = [
        dma((3,)),
        dma(()),
        dma((depth,)),
        dma(()),
        dma((n_mode - 1,)),
        dma((n_mode - 1,)),
        dma(()),
        dma((RING,)),
        dma(()),
        dma(((n_mode - 1) * (n_space // 2 + 1) + steps + CAP,)),
    ]
    mesons = pl.pallas_call(
        functools.partial(field_kernel, n_mode, n_space, blocks, times, depth),
        in_specs=[hbm] * 6,
        out_specs=vmem,
        out_shape=pltpu.VMEM((CAP, 2 * STRIP, width), bf16),
        scratch_shapes=buffers + semaphores,
        compiler_params=pltpu.CompilerParams(
            collective_id=0, has_side_effects=True, vmem_limit_bytes=limit
        ),
        name="field",
    )(
        diag_time, diag_mom, owner_list, resident.reshape(2, res_dev * times, slab),
        source.reshape(2, src_dev * times, slab), insertion,
    )
    mesons = mesons.reshape(CAP, 2, STRIP, width)
    if strip_count < slots:
        taken = jnp.sum((owner_list == me_space).astype(jnp.int32))
        filled = jnp.arange(CAP, dtype=jnp.int32) < taken
        mesons = jnp.where(filled[:, None, None, None], mesons, jnp.zeros_like(mesons))
    return mesons


def solution(mesh):
    in_specs = (
        P(None, "mode", None, "space"),
        P(None, "mode", None, "space"),
        P(),
        P("mode", None),
        P(),
        P(),
    )
    out_specs = P("space", None, "mode", None)
    return jax.shard_map(
        on_device, mesh=mesh, in_specs=in_specs, out_specs=out_specs, check_vma=False
    )
```
